32 devices in a mesh: tile: 16 (over z, y, x), vec: 2 (over core).
Axes of the slice: x: 2, y: 2, z: 4, core: 2. Of those that a mesh axis runs over, the one named last changes fastest.
Arguments:
- trial: bfloat16 [1, 1024, 1024], P(None, ('tile', 'vec')), may hold values from -0.005859375 to 0.005859375
- psi_v: bfloat16 [1024, 8192], P(None, 'tile'), may hold values from -6 to 6
- psi_c: bfloat16 [1024, 2, 4096], P(None, 'vec', 'tile'), may hold values from -6 to 6
- screened: float32 [8192, 8192], P('tile', 'vec'), may hold values from -0.0007324219 to 0.0007324219
Outputs:
- result: float32 [1, 1024, 1024], P(None, ('tile', 'vec'))
The draws below stay inside these ranges and needn't reach their ends.
All inputs are finite; a program needn't handle non-finite values.
Results may differ from the reference program's by a relative error of at most 0.0041.
Values may be sent and summed in bfloat16 or wider, within the bound.
A program may use at most 64 MiB of HBM per device.

```python
import jax
import jax.numpy as jnp
from jax import lax

NV = 1024
NC = 1024
NP = 8192
NVEC = 1
NPH = 4096
N_VEC = 2


def with_spikes(values, stream_key, source, target, blocks, factor):
    owner, partner = [(jnp.arange(values.shape[axis_at]) // (values.shape[axis_at] // blocks)).reshape([-1 if axis == axis_at else 1 for axis in range(values.ndim)]) for axis_at in (source, target)]
    chosen = jax.random.permutation(stream_key, blocks)[partner]
    strong = (owner == chosen) | (owner == (partner + blocks // 2) % blocks)
    return jnp.where(strong, factor * values, values)


def steps_of(rng, dims, cuts, smallest, largest):
    level, own = 1.0, jax.random.fold_in(rng, 6)
    for axis_at, shards_of in cuts:
        draws = jnp.exp(jax.random.uniform(jax.random.fold_in(own, axis_at), (shards_of,), jnp.float32, smallest / len(cuts), largest / len(cuts)))
        level = level * jnp.repeat(draws, dims[axis_at] // shards_of).reshape([-1 if axis == axis_at else 1 for axis in range(len(dims))])
    return level


def noise(stream_key, shape, spread, bound, cuts=(), held_as=jnp.bfloat16):
    factor_of = steps_of(stream_key, shape, cuts, -0.22, 0.18) if cuts else 1.0
    drawn = jax.random.normal(stream_key, shape, jnp.float32) * spread * factor_of
    return jnp.minimum(jnp.maximum(drawn, -bound), bound).astype(held_as)


def bell_draw_with(own_key, shape, scale, reach, pieces, heavy, kind=jnp.bfloat16):
    result = scale * jax.random.normal(own_key, shape, jnp.float32)
    if pieces:
        result = result * steps_of(own_key, shape, pieces, -0.22, 0.18)
    return jnp.clip(with_spikes(result, jax.random.fold_in(own_key, 3), *heavy), -reach, reach).astype(kind)


def setup_inputs(seed: int = 0) -> dict:
    splits = jax.random.split(jax.random.key(seed), 5)
    trial = noise(splits[0], (NVEC, NV, NC), (NV * NC) ** -0.5, 0.005859375, ((1, 32),))
    psi_v = bell_draw_with(splits[1], (NV, NP), 1.0, 6.0, ((1, 16),), (1, 0, 16, 2.0))
    psi_c = noise(splits[2], (NC, N_VEC, NPH), 1.0, 6.0, ((1, 2), (2, 16)))
    screened = noise(splits[3], (NP, NP), (NP * NP) ** -0.5, 0.0007324219, ((0, 16), (1, 2)), jnp.float32)
    return dict(trial=trial, psi_v=psi_v, psi_c=psi_c, screened=screened)


def reference(trial, psi_v, psi_c, screened):
    conduction = psi_c.reshape(NC, NP)
    left = psi_v.astype(jnp.float32)

    def one_vector(single):
        projected = jnp.dot(psi_v.T, single, preferred_element_type=jnp.float32).astype(jnp.bfloat16)
        pair = jnp.dot(projected, conduction, preferred_element_type=jnp.float32)
        weighted = (screened * pair).astype(jnp.bfloat16)
        back = jnp.dot(weighted, conduction.T, preferred_element_type=jnp.float32)
        return jnp.dot(left, back, precision=lax.Precision.HIGHEST)

    return lax.map(one_vector, trial)
```

```python
import functools

import jax
import jax.numpy as jnp
from jax import lax
from jax.experimental import pallas as pl
from jax.experimental.pallas import tpu as pltpu
from jax.sharding import PartitionSpec as P

RING = 4
CUTS = 2
EARLY = 4


def back_product(weighted_flat, panel):
    return lax.dot_general(
        weighted_flat, panel, (((1,), (1,)), ((), ())), preferred_element_type=jnp.float32
    )


def plain(trial, psi_v, psi_c, screened):
    count = trial.shape[0]
    points = psi_v.shape[1]
    conduct = trial.shape[2]
    whole = lax.all_gather(trial, ("tile", "vec"), axis=1, tiled=True)
    projected = jnp.einsum("vp,kvc->kpc", psi_v, whole, preferred_element_type=jnp.float32).astype(
        jnp.bfloat16
    )
    flat = projected.reshape(count * points, conduct)
    panel_local = psi_c[:, 0, :]
    panel = lax.all_gather(panel_local, "tile", axis=1, tiled=True)
    pair = jnp.dot(flat, panel, preferred_element_type=jnp.float32)
    weighted = (screened[None] * pair.reshape(count, points, -1)).astype(jnp.bfloat16)
    weighted_flat = weighted.reshape(count * points, -1)
    back = back_product(weighted_flat, panel)
    back = back.reshape(count, points, conduct)
    left = psi_v.astype(jnp.float32)
    summed = lax.psum(back, "vec")
    tiles = lax.axis_size("tile")
    halves = lax.axis_size("vec")
    owned = left.shape[0] // (tiles * halves)
    grouped = left.reshape(tiles, halves, owned, points)
    mine = lax.dynamic_index_in_dim(grouped, lax.axis_index("vec"), 1, keepdims=False).reshape(
        tiles * owned, points
    )
    pieces = []
    for one in range(count):
        term = jnp.dot(mine, summed[one], precision=lax.Precision.HIGHEST)
        pieces.append(lax.psum_scatter(term, "tile", scatter_dimension=0, tiled=True))
    return jnp.stack(pieces, axis=0)


def gray(r):
    return r + (r // 2) - 2 * (r // 3)


def arrivals(layers):
    near = [d for d in range(1, layers)]
    near.sort(key=lambda d: min(d, layers - d))
    order = [(0, 0)]
    first = near[:2]
    order += [(d, 0) for d in first]
    order += [(0, 1), (0, 3)]
    order += [(d, 0) for d in near[2:]]
    for d in near:
        order += [(d, 1), (d, 3)]
    order += [(d, 2) for d in [0] + near]
    return order


def body(
    tiles,
    trial_ref,
    psi_v_hbm,
    psi_c_ref,
    screened_hbm,
    out_ref,
    whole,
    psi_v,
    psi_t,
    screened,
    panel,
    flat,
    back,
    give,
    take,
    term,
    parts,
    local_sem,
    trial_send,
    trial_recv,
    hand_send,
    hand_recv,
    block_send,
    block_recv,
    back_sem,
    part_send,
    part_recv,
):
    layers = tiles // RING
    me = lax.axis_index("tile")
    half = lax.axis_index("vec")
    other = 1 - half
    a = me // RING
    r = gray(me % RING)
    order = arrivals(layers)
    slot = {event: i for i, event in enumerate(order)}

    def at(da, dr):
        return ((a + da) % layers) * RING + gray((r + dr) % RING)

    ahead, behind = at(0, 1), at(0, RING - 1)

    def remote(src, dst, send, recv, tile, vec):
        return pltpu.make_async_remote_copy(
            src_ref=src,
            dst_ref=dst,
            send_sem=send,
            recv_sem=recv,
            device_id=(tile, vec),
            device_id_type=pl.DeviceIdType.MESH,
        )

    load_psi = pltpu.make_async_copy(psi_v_hbm, psi_v, local_sem.at[0])
    load_psi.start()
    load_screened = pltpu.make_async_copy(screened_hbm, screened, local_sem.at[1])
    load_screened.start()

    barrier = pltpu.get_barrier_semaphore()
    for d in range(1, tiles):
        for v in range(2):
            pl.semaphore_signal(
                barrier,
                inc=1,
                device_id=((me + d) % tiles, v),
                device_id_type=pl.DeviceIdType.MESH,
            )
    pl.semaphore_signal(
        barrier, inc=1, device_id=(me, other), device_id_type=pl.DeviceIdType.MESH
    )
    pl.semaphore_wait(barrier, 2 * tiles - 1)

    rows = trial_ref.shape[0]

    def lines(tile, vec):
        start = pl.multiple_of((tile * 2 + vec) * rows, rows)
        return whole.at[pl.ds(start, rows), :]

    sent = []
    def hand(d, src):
        tile = (me + tiles - d) % tiles
        copy = remote(src, lines(tile, half), hand_send.at[d], hand_recv.at[d], me, other)
        copy.start()
        sent.append(copy)

    for d in range(1, tiles):
        copy = remote(
            trial_ref,
            lines(me, half),
            trial_send.at[d],
            trial_recv.at[d],
            (me + d) % tiles,
            half,
        )
        copy.start()
        sent.append(copy)
    hand(0, trial_ref)

    height = psi_c_ref.shape[0] // CUTS
    counter = [0]

    def piece(ref, s):
        return ref.at[pl.ds(s * height, height), :]

    def send_block(event, s, src, owner, tile):
        copy = remote(
            piece(src, s),
            piece(panel.at[owner], s),
            block_send.at[counter[0]],
            block_recv.at[slot[event], s],
            tile,
            half,
        )
        counter[0] += 1
        copy.start()

    for s in range(CUTS):
        send_block((0, 1), s, psi_c_ref, me, ahead)
        send_block((0, 3), s, psi_c_ref, me, behind)
        for da in range(1, layers):
            send_block((da, 0), s, psi_c_ref, me, at(da, 0))

    def owner_of(event):
        da, dr = event
        return at(layers - da, RING - dr)

    owners = {event: owner_of(event) for event in order}

    def arrive(event):
        da, dr = event
        owner = owners[event]
        for s in range(CUTS):
            ref = piece(panel.at[owner], s)
            remote(
                ref, ref, block_send.at[0], block_recv.at[slot[event], s], me, other
            ).wait_recv()
            if dr == 0:
                send_block((da, 1), s, panel.at[owner], owner, ahead)
                send_block((da, 3), s, panel.at[owner], owner, behind)
            elif dr == 1 and da % 2 == 0:
                send_block((da, 2), s, panel.at[owner], owner, ahead)
            elif dr == 3 and da % 2 == 1:
                send_block((da, 2), s, panel.at[owner], owner, behind)

    whole[pl.ds(pl.multiple_of((me * 2 + half) * rows, rows), rows), :] = trial_ref[...]
    panel[pl.ds(me, 1)] = psi_c_ref[...][None]
    back[...] = jnp.zeros_like(back)
    load_psi.wait()
    psi_t[...] = psi_v[...].T

    for d in range(1, tiles):
        tile = (me + tiles - d) % tiles
        ref = lines(tile, half)
        remote(ref, ref, trial_send.at[0], trial_recv.at[d], me, other).wait_recv()
        hand(d, ref)
    early = min(EARLY, len(order) - 1)
    for event in order[1 : early + 1]:
        arrive(event)
    for d in range(tiles):
        tile = (me + tiles - d) % tiles
        ref = lines(tile, other)
        remote(ref, ref, hand_send.at[0], hand_recv.at[d], me, other).wait_recv()

    conduct = whole.shape[1]
    wide = 256

    def project(j, carry):
        columns = pl.ds(pl.multiple_of(j * wide, wide), wide)
        flat[:, columns] = jnp.dot(
            psi_t[...], whole[:, columns], preferred_element_type=jnp.float32
        ).astype(jnp.bfloat16)
        return carry

    lax.fori_loop(0, conduct // wide, project, 0)
    load_screened.wait()

    width = psi_c_ref.shape[1]
    middle = conduct // 2

    def use(k, carry):
        owner = me
        for i, event in enumerate(order):
            if i > early:

                @pl.when(k == i)
                def _(event=event):
                    arrive(event)

            owner = jnp.where(k == i, owners[event], owner)
        block = panel.at[owner]
        pair = jnp.dot(flat[...], block[...], preferred_element_type=jnp.float32)
        columns = pl.ds(pl.multiple_of(owner * width, 128), width)
        weighted = (screened[:, columns] * pair).astype(jnp.bfloat16)
        for h in range(2):
            back[h] += back_product(weighted, block[pl.ds(h * middle, middle), :])
        return carry

    lax.fori_loop(0, tiles, use, 0)

    give[...] = back[other].astype(jnp.bfloat16)
    swap = remote(give, take, back_sem.at[0], back_sem.at[1], me, other)
    swap.start()
    swap.wait()
    total = back[half] + take[...].astype(jnp.float32)
    high = total.astype(jnp.bfloat16)
    low = (total - high.astype(jnp.float32)).astype(jnp.bfloat16)
    flat[:, :middle] = high
    flat[:, middle:] = low
    span = 2 * rows
    step = psi_v.shape[0] // 4

    def finish(j, carry):
        lines_of = pl.ds(pl.multiple_of(j * step, step), step)
        left = psi_v[lines_of, :]
        term[lines_of, :] = (
            jnp.dot(left, flat[:, :middle], preferred_element_type=jnp.float32)
            + jnp.dot(left, flat[:, middle:], preferred_element_type=jnp.float32)
        ).astype(jnp.bfloat16)
        return carry

    lax.fori_loop(0, 4, finish, 0)

    def owned(tile, vec):
        return pl.ds(pl.multiple_of(tile * span + vec * rows, rows), rows)

    for d in list(range(1, tiles)) + [0]:
        for flip in range(2):
            if d == 0 and flip == 0:
                continue
            tile = (me + d) % tiles
            vec = (half + flip) % 2
            copy = remote(
                term.at[owned(tile, vec), :],
                parts.at[me, half],
                part_send.at[d, flip],
                part_recv.at[d, flip],
                tile,
                vec,
            )
            copy.start()
            sent.append(copy)
    sums = [term[owned(me, half), :].astype(jnp.float32), None]
    for d in [0] + list(range(1, tiles)):
        for flip in range(2):
            if d == 0 and flip == 0:
                continue
            ref = parts.at[(me + tiles - d) % tiles, (half + flip) % 2]
            remote(ref, ref, part_send.at[0, 0], part_recv.at[d, flip], me, other).wait_recv()
            value = ref[...].astype(jnp.float32)
            sums[flip] = value if sums[flip] is None else sums[flip] + value
    for flip in range(2):
        place = (half + flip) % 2
        out_ref[:, pl.ds(pl.multiple_of(place * middle, 128), middle)] = sums[flip]
    for copy in sent:
        copy.wait_send()
    for i in range(counter[0]):
        ref = piece(psi_c_ref, 0)
        remote(ref, ref, block_send.at[i], block_recv.at[0, 0], me, other).wait_send()


def fused(tiles, trial, psi_v, psi_c, screened):
    rows, conduct = trial.shape[1:]
    valence, points = psi_v.shape
    width = psi_c.shape[2]
    middle = conduct // 2
    bf16, f32 = jnp.bfloat16, jnp.float32
    vmem = pl.BlockSpec(memory_space=pltpu.VMEM)
    far = pl.BlockSpec(memory_space=pl.ANY)
    dma = pltpu.SemaphoreType.DMA
    out = pl.pallas_call(
        functools.partial(body, tiles),
        out_shape=jax.ShapeDtypeStruct((rows, conduct), f32),
        in_specs=[vmem, far, vmem, far],
        out_specs=vmem,
        scratch_shapes=[
            pltpu.VMEM((valence, conduct), bf16),
            pltpu.VMEM((valence, points), bf16),
            pltpu.VMEM((points, valence), bf16),
            pltpu.VMEM(screened.shape, f32),
            pltpu.VMEM((tiles, conduct, width), bf16),
            pltpu.VMEM((points, conduct), bf16),
            pltpu.VMEM((2, points, middle), f32),
            pltpu.VMEM((points, middle), bf16),
            pltpu.VMEM((points, middle), bf16),
            pltpu.VMEM((valence, middle), bf16),
            pltpu.VMEM((tiles, 2, rows, middle), bf16),
            dma((2,)),
            dma((tiles,)),
            dma((tiles,)),
            dma((tiles,)),
            dma((tiles,)),
            dma((tiles * CUTS,)),
            dma((tiles, CUTS)),
            dma((2,)),
            dma((tiles, 2)),
            dma((tiles, 2)),
        ],
        compiler_params=pltpu.CompilerParams(
            collective_id=0, has_side_effects=True, vmem_limit_bytes=58 * 1024 * 1024
        ),
    )(trial[0], psi_v, psi_c[:, 0, :], screened)
    return out[None]


def solution(mesh):
    tiles = mesh.shape["tile"]

    def shards(trial, psi_v, psi_c, screened):
        fits = (
            trial.shape[0] == 1
            and mesh.shape["vec"] == 2
            and tiles % RING == 0
            and psi_c.shape[2] % 128 == 0
            and trial.shape[1] % 16 == 0
            and trial.shape[2] % 256 == 0
        )
        if fits:
            return fused(tiles, trial, psi_v, psi_c, screened)
        return plain(trial, psi_v, psi_c, screened)

    in_specs = (
        P(None, ("tile", "vec"), None),
        P(None, "tile"),
        P(None, "vec", "tile"),
        P("tile", "vec"),
    )
    out_specs = P(None, ("tile", "vec"), None)
    return jax.shard_map(shards, mesh=mesh, in_specs=in_specs, out_specs=out_specs, check_vma=False)
```

```python
import functools

import jax
import jax.numpy as jnp
from jax import lax
from jax.experimental import pallas as pl
from jax.experimental.pallas import tpu as pltpu
from jax.sharding import PartitionSpec as P

RING = 4
CUTS = 4
EARLY = 3


def back_product(weighted_flat, panel):
    return lax.dot_general(
        weighted_flat, panel, (((1,), (1,)), ((), ())), preferred_element_type=jnp.float32
    )


def plain(trial, psi_v, psi_c, screened):
    count = trial.shape[0]
    points = psi_v.shape[1]
    conduct = trial.shape[2]
    whole = lax.all_gather(trial, ("tile", "vec"), axis=1, tiled=True)
    projected = jnp.einsum("vp,kvc->kpc", psi_v, whole, preferred_element_type=jnp.float32).astype(
        jnp.bfloat16
    )
    flat = projected.reshape(count * points, conduct)
    panel_local = psi_c[:, 0, :]
    panel = lax.all_gather(panel_local, "tile", axis=1, tiled=True)
    pair = jnp.dot(flat, panel, preferred_element_type=jnp.float32)
    weighted = (screened[None] * pair.reshape(count, points, -1)).astype(jnp.bfloat16)
    weighted_flat = weighted.reshape(count * points, -1)
    back = back_product(weighted_flat, panel)
    back = back.reshape(count, points, conduct)
    left = psi_v.astype(jnp.float32)
    summed = lax.psum(back, "vec")
    tiles = lax.axis_size("tile")
    halves = lax.axis_size("vec")
    owned = left.shape[0] // (tiles * halves)
    grouped = left.reshape(tiles, halves, owned, points)
    mine = lax.dynamic_index_in_dim(grouped, lax.axis_index("vec"), 1, keepdims=False).reshape(
        tiles * owned, points
    )
    pieces = []
    for one in range(count):
        term = jnp.dot(mine, summed[one], precision=lax.Precision.HIGHEST)
        pieces.append(lax.psum_scatter(term, "tile", scatter_dimension=0, tiled=True))
    return jnp.stack(pieces, axis=0)


def gray(r):
    return r + (r // 2) - 2 * (r // 3)


def flip_bits(a, mask):
    bit = 1
    while bit <= mask:
        if mask & bit:
            a = a + bit - 2 * bit * ((a // bit) % 2)
        bit *= 2
    return a


def arrivals(layers):
    near = [d for d in [1] + list(range(layers - 1, 1, -1)) if d < layers]
    order = [(0, 0)]
    order += [(d, 0) for d in near[:1]]
    order += [(0, 1), (0, 3)]
    for d in near[:1]:
        order += [(d, 3), (d, 1)]
    order += [(d, 0) for d in near[1:2]]
    order += [(0, 2)]
    order += [(d, 0) for d in near[2:]]
    for d in near[1:]:
        order += [(d, 3), (d, 1)]
    order += [(d, 2) for d in near]
    return near, order


def body(
    tiles,
    trial_ref,
    psi_v_hbm,
    psi_c_ref,
    screened_hbm,
    out_ref,
    whole,
    psi_v,
    psi_t,
    screened,
    panel,
    flat,
    back,
    give,
    take,
    term,
    parts,
    local_sem,
    trial_send,
    trial_recv,
    hand_send,
    hand_recv,
    block_send,
    block_recv,
    back_sem,
    part_send,
    part_recv,
):
    layers = tiles // RING
    me = lax.axis_index("tile")
    half = lax.axis_index("vec")
    other = 1 - half
    a = me // RING
    r = gray(me % RING)
    near, order = arrivals(layers)
    slot = {event: i for i, event in enumerate(order)}

    def at(da, dr):
        return flip_bits(a, da) * RING + gray((r + dr) % RING)

    columns_of = {d: at(d, 0) for d in range(1, layers)}
    ahead, behind = at(0, 1), at(0, RING - 1)

    def remote(src, dst, send, recv, tile, vec):
        return pltpu.make_async_remote_copy(
            src_ref=src,
            dst_ref=dst,
            send_sem=send,
            recv_sem=recv,
            device_id=(tile, vec),
            device_id_type=pl.DeviceIdType.MESH,
        )

    load_psi = pltpu.make_async_copy(psi_v_hbm, psi_v, local_sem.at[0])
    load_psi.start()
    load_screened = pltpu.make_async_copy(screened_hbm, screened, local_sem.at[1])
    load_screened.start()

    barrier = pltpu.get_barrier_semaphore()
    for d in range(1, tiles):
        for v in range(2):
            pl.semaphore_signal(
                barrier,
                inc=1,
                device_id=((me + d) % tiles, v),
                device_id_type=pl.DeviceIdType.MESH,
            )
    pl.semaphore_signal(
        barrier, inc=1, device_id=(me, other), device_id_type=pl.DeviceIdType.MESH
    )
    pl.semaphore_wait(barrier, 2 * tiles - 1)

    rows = trial_ref.shape[0]

    def lines(tile, vec):
        start = pl.multiple_of((tile * 2 + vec) * rows, rows)
        return whole.at[pl.ds(start, rows), :]

    def owner_of(event):
        da, dr = event
        return at(da, (RING - dr) % RING)

    owners = {event: owner_of(event) for event in order}

    def targets(event):
        da, dr = event
        if event == (0, 0):
            return [((0, 1), ahead), ((0, 3), behind)] + [((d, 0), at(d, 0)) for d in near]
        if dr == 0:
            return [((da, 1), ahead), ((da, 3), behind)]
        if dr == 1 and da % 2 == 0:
            return [((da, 2), ahead)]
        if dr == 3 and da % 2 == 1:
            return [((da, 2), behind)]
        return []

    sent = []

    def pass_on(event, src):
        owner = owners[event]
        d = slot[event]
        for later, tile in targets(event):
            i = slot[later]
            copy = remote(src, lines(owner, half), trial_send.at[i], trial_recv.at[i], tile, half)
            copy.start()
            sent.append(copy)
        copy = remote(src, lines(owner, half), hand_send.at[d], hand_recv.at[d], me, other)
        copy.start()
        sent.append(copy)

    def take_rows(event):
        ref = lines(owners[event], half)
        remote(ref, ref, trial_send.at[0], trial_recv.at[slot[event]], me, other).wait_recv()
        pass_on(event, ref)

    pass_on((0, 0), trial_ref)

    height = psi_c_ref.shape[0] // CUTS
    counter = [0]

    def piece(ref, s):
        return ref.at[pl.ds(s * height, height), :]

    def send_block(event, s, src, owner, tile):
        copy = remote(
            piece(src, s),
            piece(panel.at[owner], s),
            block_send.at[counter[0]],
            block_recv.at[slot[event], s],
            tile,
            half,
        )
        counter[0] += 1
        copy.start()

    for d in near:
        for s in range(CUTS):
            send_block((d, 0), s, psi_c_ref, me, at(d, 0))

    def arrive(event):
        owner = owners[event]
        for s in range(CUTS):
            ref = piece(panel.at[owner], s)
            remote(
                ref, ref, block_send.at[0], block_recv.at[slot[event], s], me, other
            ).wait_recv()
            onward = targets(event)
            if s == CUTS - 1 and event == (0, 2):
                onward = [((d, 2), columns_of[d]) for d in near]
            elif s == CUTS - 1 and event[0] != 0 and event[1] != 0:
                onward = []
            for later, tile in onward:
                send_block(later, s, panel.at[owner], owner, tile)

    early = min(EARLY, len(order) - 1)
    for d in near:
        take_rows((d, 0))
    for s in range(CUTS):
        send_block((0, 1), s, psi_c_ref, me, ahead)
        send_block((0, 3), s, psi_c_ref, me, behind)
    whole[pl.ds(pl.multiple_of((me * 2 + half) * rows, rows), rows), :] = trial_ref[...]
    panel[pl.ds(me, 1)] = psi_c_ref[...][None]
    back[...] = jnp.zeros_like(back)
    load_psi.wait()
    psi_t[...] = psi_v[...].T

    for event in order[1:]:
        if event[1] in (1, 3):
            take_rows(event)
    for event in order[1 : early + 1]:
        arrive(event)
    for event in order[1:]:
        if event[1] == 2:
            take_rows(event)
    for event in order:
        ref = lines(owners[event], other)
        remote(ref, ref, hand_send.at[0], hand_recv.at[slot[event]], me, other).wait_recv()

    conduct = whole.shape[1]
    wide = 256

    def project(j, carry):
        columns = pl.ds(pl.multiple_of(j * wide, wide), wide)
        flat[:, columns] = jnp.dot(
            psi_t[...], whole[:, columns], preferred_element_type=jnp.float32
        ).astype(jnp.bfloat16)
        return carry

    lax.fori_loop(0, conduct // wide, project, 0)
    load_screened.wait()

    width = psi_c_ref.shape[1]
    middle = conduct // 2

    def use(k, carry):
        owner = me
        for i, event in enumerate(order):
            if i > early:

                @pl.when(k == i)
                def _(event=event):
                    arrive(event)

            owner = jnp.where(k == i, owners[event], owner)
        block = panel.at[owner]
        pair = jnp.dot(flat[...], block[...], preferred_element_type=jnp.float32)
        columns = pl.ds(pl.multiple_of(owner * width, 128), width)
        weighted = (screened[:, columns] * pair).astype(jnp.bfloat16)
        for h in range(2):
            back[h] += back_product(weighted, block[pl.ds(h * middle, middle), :])
        return carry

    lax.fori_loop(0, tiles, use, 0)

    give[...] = back[other].astype(jnp.bfloat16)
    swap = remote(give, take, back_sem.at[0], back_sem.at[1], me, other)
    swap.start()
    swap.wait()
    total = back[half] + take[...].astype(jnp.float32)
    high = total.astype(jnp.bfloat16)
    low = (total - high.astype(jnp.float32)).astype(jnp.bfloat16)
    flat[:, :middle] = high
    flat[:, middle:] = low
    span = 2 * rows
    step = psi_v.shape[0] // 4

    def finish(j, carry):
        lines_of = pl.ds(pl.multiple_of(j * step, step), step)
        left = psi_v[lines_of, :]
        term[lines_of, :] = (
            jnp.dot(left, flat[:, :middle], preferred_element_type=jnp.float32)
            + jnp.dot(left, flat[:, middle:], preferred_element_type=jnp.float32)
        ).astype(jnp.bfloat16)
        return carry

    lax.fori_loop(0, 4, finish, 0)

    def owned(tile, vec):
        return pl.ds(pl.multiple_of(tile * span + vec * rows, rows), rows)

    for d in list(range(1, tiles)) + [0]:
        for flip in range(2):
            if d == 0 and flip == 0:
                continue
            tile = (me + d) % tiles
            vec = (half + flip) % 2
            copy = remote(
                term.at[owned(tile, vec), :],
                parts.at[me, half],
                part_send.at[d, flip],
                part_recv.at[d, flip],
                tile,
                vec,
            )
            copy.start()
            sent.append(copy)
    sums = [term[owned(me, half), :].astype(jnp.float32), None]
    for d in [0] + list(range(1, tiles)):
        for flip in range(2):
            if d == 0 and flip == 0:
                continue
            ref = parts.at[(me + tiles - d) % tiles, (half + flip) % 2]
            remote(ref, ref, part_send.at[0, 0], part_recv.at[d, flip], me, other).wait_recv()
            value = ref[...].astype(jnp.float32)
            sums[flip] = value if sums[flip] is None else sums[flip] + value
    for flip in range(2):
        place = (half + flip) % 2
        out_ref[:, pl.ds(pl.multiple_of(place * middle, 128), middle)] = sums[flip]
    for copy in sent:
        copy.wait_send()
    for i in range(counter[0]):
        ref = piece(psi_c_ref, 0)
        remote(ref, ref, block_send.at[i], block_recv.at[0, 0], me, other).wait_send()


def fused(tiles, trial, psi_v, psi_c, screened):
    rows, conduct = trial.shape[1:]
    valence, points = psi_v.shape
    width = psi_c.shape[2]
    middle = conduct // 2
    bf16, f32 = jnp.bfloat16, jnp.float32
    vmem = pl.BlockSpec(memory_space=pltpu.VMEM)
    far = pl.BlockSpec(memory_space=pl.ANY)
    dma = pltpu.SemaphoreType.DMA
    out = pl.pallas_call(
        functools.partial(body, tiles),
        out_shape=jax.ShapeDtypeStruct((rows, conduct), f32),
        in_specs=[vmem, far, vmem, far],
        out_specs=vmem,
        scratch_shapes=[
            pltpu.VMEM((valence, conduct), bf16),
            pltpu.VMEM((valence, points), bf16),
            pltpu.VMEM((points, valence), bf16),
            pltpu.VMEM(screened.shape, f32),
            pltpu.VMEM((tiles, conduct, width), bf16),
            pltpu.VMEM((points, conduct), bf16),
            pltpu.VMEM((2, points, middle), f32),
            pltpu.VMEM((points, middle), bf16),
            pltpu.VMEM((points, middle), bf16),
            pltpu.VMEM((valence, middle), bf16),
            pltpu.VMEM((tiles, 2, rows, middle), bf16),
            dma((2,)),
            dma((tiles,)),
            dma((tiles,)),
            dma((tiles,)),
            dma((tiles,)),
            dma((tiles * CUTS,)),
            dma((tiles, CUTS)),
            dma((2,)),
            dma((tiles, 2)),
            dma((tiles, 2)),
        ],
        compiler_params=pltpu.CompilerParams(
            collective_id=0, has_side_effects=True, vmem_limit_bytes=58 * 1024 * 1024
        ),
    )(trial[0], psi_v, psi_c[:, 0, :], screened)
    return out[None]


def solution(mesh):
    tiles = mesh.shape["tile"]

    def shards(trial, psi_v, psi_c, screened):
        fits = (
            trial.shape[0] == 1
            and mesh.shape["vec"] == 2
            and tiles % RING == 0
            and (tiles & (tiles - 1)) == 0
            and psi_c.shape[2] % 128 == 0
            and trial.shape[1] % 16 == 0
            and trial.shape[2] % 256 == 0
        )
        if fits:
            return fused(tiles, trial, psi_v, psi_c, screened)
        return plain(trial, psi_v, psi_c, screened)

    in_specs = (
        P(None, ("tile", "vec"), None),
        P(None, "tile"),
        P(None, "vec", "tile"),
        P("tile", "vec"),
    )
    out_specs = P(None, ("tile", "vec"), None)
    return jax.shard_map(shards, mesh=mesh, in_specs=in_specs, out_specs=out_specs, check_vma=False)
```
